32 devices in a mesh: rep: 4 (over x, core), ep: 4 (over z), grp: 2 (over y).
Axes of the slice: x: 2, y: 2, z: 4, core: 2. Of those that a mesh axis runs over, the one named last changes fastest.
Arguments:
- tokens: bfloat16 [4096, 2048], P(('rep', 'ep', 'grp')), may hold values from -6 to 6
- grad_out: bfloat16 [4096, 2048], P(('rep', 'ep', 'grp')), may hold values from -6 to 6
- expert_ids: int32 [4096, 2], P(('rep', 'ep', 'grp')), may hold values from 0 to 7, as said below
- combine: bfloat16 [4096, 2], P(('rep', 'ep', 'grp')), may hold values from 0.099609375 to 1
- weights: bfloat16 [2048, 3, 7168], P('grp', None, 'ep'), may hold values from -0.125 to 0.125
Outputs:
- grad_tokens: bfloat16 [4096, 2048], P(('rep', 'ep', 'grp'))
- grad_combine: float32 [4096, 2], P(('rep', 'ep', 'grp'))
- grad_weights: float32 [2048, 3, 7168], P(('rep', 'grp'), None, 'ep')
The draws below stay inside these ranges and needn't reach their ends.
Inputs may be any that keep to these rules, and one draw needn't show every extreme that they name: `expert_ids`: each token names 2 different experts, at most one of them below 1. No expert below 1 is named by more than 4 tokens of one device, and each of them is named by exactly 4 tokens of some device.
All inputs are finite; a program needn't handle non-finite values.
Results may differ from the reference program's by a relative error of at most 0.0085.
Values may be sent and summed in bfloat16 or wider, within the bound.
A program may use at most 128 MiB of HBM per device.

```python
import jax
import jax.numpy as jnp
from jax import lax

D = 2048
FF = 7168
EXPERTS = 8
TOPK = 2
FLIGHT = 1
TOK_DEV = 128
CAP = 4
TOKENS = 4096
N_REP = 4
N_EP = 4
N_GRP = 2
DEVICES = 32


def draw_expert_ids(key, part):
    keys = jax.random.split(jax.random.fold_in(key, 7001), 6)
    blocks = DEVICES
    rows = TOK_DEV
    scores = jax.random.randint(keys[0], (blocks, rows), 0, 1 << 20) * rows + jnp.arange(rows, dtype=jnp.int32)[None, :]
    order = jnp.argsort(scores, axis=1)
    rank = jnp.argsort(order, axis=1).astype(jnp.int32)
    counts = jax.random.randint(keys[1], (blocks, FLIGHT), 0, CAP + 1)
    forced = jax.random.randint(keys[2], (FLIGHT,), 0, blocks)
    block_index = jnp.arange(blocks, dtype=jnp.int32)
    counts = jnp.where(block_index[:, None] == forced[None, :], CAP, counts).astype(jnp.int32)
    bounds = jnp.cumsum(counts, axis=1)
    lower = bounds - counts
    hits = (rank[:, :, None] >= lower[:, None, :]) & (rank[:, :, None] < bounds[:, None, :])
    hit_int = hits.astype(jnp.int32)
    chosen = jnp.sum(hit_int, axis=2) > 0
    flight_id = jnp.sum(hit_int * jnp.arange(FLIGHT, dtype=jnp.int32)[None, None, :], axis=2)
    others = EXPERTS - FLIGHT
    first = jax.random.randint(keys[3], (blocks, rows), 0, others)
    second = (first + jax.random.randint(keys[4], (blocks, rows), 1, others)) % others
    first = first + FLIGHT
    second = second + FLIGHT
    column_a = jnp.where(chosen, flight_id, first)
    column_b = jnp.where(chosen, first, second)
    flipped = jax.random.randint(keys[5], (blocks, rows), 0, 2) == 1
    left = jnp.where(flipped, column_b, column_a)
    right = jnp.where(flipped, column_a, column_b)
    return jnp.stack([left, right], axis=-1).reshape(TOKENS, TOPK).astype(jnp.int32)


def shard_levels(key, extent, shards, smallest, largest):
    gain = 1.0
    for axis_at, shards_of in shards:
        heights = jax.random.uniform(jax.random.fold_in(jax.random.fold_in(key, 6), axis_at), (shards_of,), jnp.float32, smallest / len(shards), largest / len(shards))
        gain = gain * jnp.repeat(jnp.exp(heights), extent[axis_at] // shards_of).reshape((-1,) + (1,) * (len(extent) - 1 - axis_at))
    return gain


def gaussian(key, shape, spread, most, pieces=(), kind=jnp.bfloat16):
    gain = shard_levels(key, shape, pieces, -0.22, 0.18) if pieces else 1.0
    drawn = jax.random.normal(key, shape, jnp.float32) * spread * gain
    return jnp.minimum(jnp.maximum(drawn, -most), most).astype(kind)


def setup_inputs(seed: int = 0) -> dict:
    arg_keys = jax.random.split(jax.random.key(seed), 6)
    tokens = gaussian(arg_keys[0], (TOKENS, D), 1.0, 6.0, ((0, 32),))
    grad_out = gaussian(arg_keys[1], (TOKENS, D), 1.0, 6.0, ((0, 32),))
    expert_ids = draw_expert_ids(jax.random.fold_in(arg_keys[5], 71), 0)
    combine = jnp.clip(0.099609375 + 0.9003906 * jax.random.uniform(arg_keys[3], (TOKENS, TOPK), jnp.float32) ** shard_levels(arg_keys[3], (TOKENS, TOPK), ((0, 32),), -0.2, 0.2), 0.099609375, 1.0).astype(jnp.bfloat16)
    weights = gaussian(arg_keys[4], (D, 3, FLIGHT * FF), D ** -0.5, 0.125, ((0, 2), (2, 4)))
    return dict(tokens=tokens, grad_out=grad_out, expert_ids=expert_ids, combine=combine, weights=weights)


def route_slots(routing, gate_vals, in_flight, capacity):
    experts = jnp.arange(in_flight, dtype=jnp.int32)
    matches = (routing[None, :, :] == experts[:, None, None]).astype(jnp.float32)
    assigned = jnp.sum(matches, axis=2)
    combined = jnp.sum(matches * gate_vals.astype(jnp.float32)[None, :, :], axis=2)
    before = jnp.cumsum(assigned, axis=1) - assigned
    slot_index = jnp.arange(capacity, dtype=jnp.float32)
    slot_map = (before[:, None, :] == slot_index[None, :, None]).astype(jnp.float32) * assigned[:, None, :]
    return matches, combined, slot_map


def rounded(values):
    return lax.optimization_barrier(values.astype(jnp.bfloat16)).astype(jnp.float32)


def reference(tokens, grad_out, expert_ids, combine, weights):
    quarter = N_EP // FLIGHT
    hidden = FF // quarter
    slot_total = N_EP * CAP
    highest = lax.Precision.HIGHEST

    def regroup(values):
        trailing = values.shape[1:]
        shaped = values.reshape((N_REP, N_EP, N_GRP, TOK_DEV) + trailing)
        return jnp.moveaxis(shaped, 2, 1)

    def ungroup(values):
        trailing = values.shape[4:]
        reordered = jnp.moveaxis(values, 1, 2)
        return reordered.reshape((N_REP * N_EP * N_GRP * TOK_DEV,) + trailing)

    split_weights = weights.reshape(D, 3, FLIGHT, FF)

    def one_group(accumulated, blocks):
        token_block, grad_block, routing, gate_vals = blocks
        matches, combined, slot_map = jax.vmap(lambda ids_one, vals_one: route_slots(ids_one, vals_one, FLIGHT, CAP))(routing, gate_vals)
        sent_rows = jnp.einsum("sfct,std->fscd", slot_map, token_block.astype(jnp.float32), precision=highest).astype(jnp.bfloat16)
        sent_grads = jnp.einsum("sfct,std->fscd", slot_map, grad_block.astype(jnp.float32), precision=highest).astype(jnp.bfloat16)
        sent_scale = jnp.einsum("sfct,sft->fsc", slot_map, combined, precision=highest)
        grad_tok = jnp.zeros((N_EP, TOK_DEV, D), jnp.float32)
        per_list = []
        term_list = []
        for expert in range(FLIGHT):
            token_rows = sent_rows[expert].reshape(slot_total, D)
            grad_rows = sent_grads[expert].reshape(slot_total, D)
            row_scale = sent_scale[expert].reshape(slot_total, 1)
            gate_pre = jnp.dot(token_rows, split_weights[:, 0, expert], preferred_element_type=jnp.float32)
            up_pre = jnp.dot(token_rows, split_weights[:, 1, expert], preferred_element_type=jnp.float32)
            down_back = jnp.dot(grad_rows, split_weights[:, 2, expert], preferred_element_type=jnp.float32)
            sigmoid_gate = jax.nn.sigmoid(gate_pre)
            activated = gate_pre * sigmoid_gate
            hid_value = activated * up_pre
            hid_grad = row_scale * down_back
            grad_gate = (hid_grad * up_pre * sigmoid_gate * (1.0 + gate_pre * (1.0 - sigmoid_gate))).astype(jnp.bfloat16)
            grad_up = (hid_grad * activated).astype(jnp.bfloat16)
            scaled_hid = (row_scale * hid_value).astype(jnp.bfloat16)
            gate_up_grad = jnp.stack([grad_gate, grad_up], axis=1).astype(jnp.float32)
            sliced_grad = gate_up_grad.reshape(slot_total, 2, quarter, hidden)
            sliced_weight = split_weights[:, :2, expert].astype(jnp.float32).reshape(D, 2, quarter, hidden)
            partial_x = jnp.einsum("rkqh,dkqh->qrd", sliced_grad, sliced_weight)
            summed_x = jnp.sum(rounded(partial_x), axis=0)
            partial_c = jnp.sum((hid_value * down_back).reshape(slot_total, quarter, hidden), axis=2)
            summed_c = jnp.sum(rounded(partial_c), axis=1)
            grad_tok = grad_tok + jnp.einsum("sct,scd->std", slot_map[:, expert], summed_x.reshape(N_EP, CAP, D), precision=highest)
            per_list.append(jnp.einsum("sct,sc->st", slot_map[:, expert], summed_c.reshape(N_EP, CAP), precision=highest))
            gate_up_term = jnp.einsum("rd,rkf->dkf", token_rows.astype(jnp.float32), gate_up_grad)
            down_term = jnp.dot(grad_rows.T, scaled_hid, preferred_element_type=jnp.float32)
            term_list.append(jnp.concatenate([gate_up_term, down_term[:, None, :]], axis=1))
        group_term = jnp.stack(term_list, axis=2)
        per_token = jnp.stack(per_list, axis=1)
        grad_gates = jnp.sum(matches * per_token[:, :, :, None], axis=1)
        return accumulated + group_term, (grad_tok.astype(jnp.bfloat16), grad_gates)

    def one_rep(total, rep_blocks):
        start = jnp.zeros((D, 3, FLIGHT, FF), jnp.float32)
        rep_sum, outputs = lax.scan(one_group, start, rep_blocks)
        return total + rounded(rep_sum), outputs

    initial = jnp.zeros((D, 3, FLIGHT, FF), jnp.float32)
    inputs_group = (regroup(tokens), regroup(grad_out), regroup(expert_ids), regroup(combine))
    accumulated, outputs_group = lax.scan(one_rep, initial, inputs_group)
    grad_tokens = ungroup(outputs_group[0])
    grad_combine = ungroup(outputs_group[1])
    return grad_tokens, grad_combine, accumulated.reshape(D, 3, FLIGHT * FF)
```

```python
import jax
import jax.numpy as jnp
from jax import lax
from jax.sharding import PartitionSpec as P

FLIGHT = 1
CAP = 4


def route_slots(routing, gate_vals):
    match = (routing == 0).astype(jnp.float32)
    assigned = jnp.sum(match, axis=1)
    combined = jnp.sum(match * gate_vals.astype(jnp.float32), axis=1)
    before = jnp.cumsum(assigned) - assigned
    slot_index = jnp.arange(CAP, dtype=jnp.float32)
    slot_map = (before[None, :] == slot_index[:, None]).astype(jnp.float32) * assigned[None, :]
    return match, combined, slot_map


def local(tokens, grad_out, expert_ids, combine, weights):
    ep, rep, grp = lax.axis_size("ep"), lax.axis_size("rep"), lax.axis_size("grp")
    me_g = lax.axis_index("grp")
    width = tokens.shape[1]
    half = width // grp
    owner = width // (rep * grp)
    hid = weights.shape[2]
    peers = ep * grp
    rows = peers * CAP
    pad = 128
    f32, bf16 = jnp.float32, jnp.bfloat16
    match, combined, slot_map = route_slots(expert_ids, combine)
    slot_bf = slot_map.astype(bf16)
    xs = jnp.dot(slot_bf, tokens, preferred_element_type=f32).astype(bf16)
    ys = jnp.dot(slot_bf, grad_out, preferred_element_type=f32).astype(bf16)
    cs = jnp.sum(slot_map * combined[None, :], axis=1).astype(bf16)
    sent = jnp.concatenate([xs, ys, jnp.broadcast_to(cs[:, None], (CAP, pad))], axis=1)
    got = lax.all_gather(sent, ("grp", "ep"), axis=0, tiled=True)
    pair = got[:, : 2 * width].reshape(rows, 2, width)
    scale = got[:, 2 * width : 2 * width + 1].astype(f32)
    mine = lax.dynamic_slice_in_dim(pair, me_g * half, half, axis=2)
    blocks = pair.reshape(rows, 2, rep, grp, owner)
    blocks = lax.dynamic_index_in_dim(blocks, me_g, axis=3, keepdims=False)
    blocks = jnp.transpose(blocks, (2, 0, 1, 3)).reshape(rep, rows, 2 * owner)
    cols = lax.all_to_all(blocks, "rep", split_axis=0, concat_axis=0, tiled=True)
    cols = cols.reshape(rep * rows, 2, owner)
    w = jnp.transpose(weights, (1, 0, 2))
    pre = jnp.concatenate(
        [
            jnp.dot(mine[:, 0], w[0], preferred_element_type=f32),
            jnp.dot(mine[:, 0], w[1], preferred_element_type=f32),
            jnp.dot(mine[:, 1], w[2], preferred_element_type=f32),
        ],
        axis=1,
    )
    pre = lax.psum(pre, "grp")
    a, b, back = pre[:, :hid], pre[:, hid : 2 * hid], pre[:, 2 * hid :]
    sig = jax.nn.sigmoid(a)
    act = a * sig
    h = act * b
    dh = scale * back
    da = (dh * b * sig * (1.0 + a * (1.0 - sig))).astype(bf16)
    db = (dh * act).astype(bf16)
    hc = (scale * h).astype(bf16)
    pc = jnp.sum(h * back, axis=1, keepdims=True).astype(bf16)
    hidden = lax.all_gather(jnp.concatenate([da, db, hc], axis=1), "rep", axis=0, tiled=True)
    dn = (((1,), (1,)), ((), ()))
    px = lax.dot_general(da, w[0], dn, preferred_element_type=f32)
    px = (px + lax.dot_general(db, w[1], dn, preferred_element_type=f32)).astype(bf16)
    out = jnp.concatenate([px, jnp.broadcast_to(pc, (rows, pad))], axis=1)
    ret = lax.all_to_all(out, ("grp", "ep"), split_axis=0, concat_axis=0, tiled=True)
    ret = ret.reshape(grp, ep, CAP, half + pad).astype(f32)
    summed = jnp.sum(ret, axis=1)
    summed_x = jnp.transpose(summed[:, :, :half], (1, 0, 2)).reshape(CAP, width)
    summed_c = summed[0, :, half]
    highest = lax.Precision.HIGHEST
    tn = (((0,), (0,)), ((), ()))
    grad_tokens = lax.dot_general(slot_map, summed_x, tn, precision=highest).astype(bf16)
    per_token = jnp.sum(slot_map * summed_c[:, None], axis=0)
    grad_combine = match * per_token[:, None]
    gw = [
        lax.dot_general(cols[:, i], hidden[:, k * hid : (k + 1) * hid], tn, preferred_element_type=f32)
        for k, i in ((0, 0), (1, 0), (2, 1))
    ]
    return grad_tokens, grad_combine, jnp.stack(gw, axis=1)


def solution(mesh):
    split = P(("rep", "ep", "grp"), None)
    in_specs = (split, split, split, split, P("grp", None, "ep"))
    out_specs = (split, split, P(("rep", "grp"), None, "ep"))
    return jax.shard_map(local, mesh=mesh, in_specs=in_specs, out_specs=out_specs, check_vma=False)
```

```python
import functools

import jax
import jax.numpy as jnp
from jax import lax
from jax.experimental import pallas as pl
from jax.experimental.pallas import tpu as pltpu
from jax.sharding import PartitionSpec as P

FLIGHT = 1
CAP = 4


def route_slots(routing, gate_vals):
    match = (routing == 0).astype(jnp.float32)
    assigned = jnp.sum(match, axis=1)
    combined = jnp.sum(match * gate_vals.astype(jnp.float32), axis=1)
    before = jnp.cumsum(assigned) - assigned
    slot_index = jnp.arange(CAP, dtype=jnp.float32)
    slot_map = (before[None, :] == slot_index[:, None]).astype(jnp.float32) * assigned[None, :]
    return match, combined, slot_map


def local(tokens, grad_out, expert_ids, combine, weights):
    ep, rep, grp = lax.axis_size("ep"), lax.axis_size("rep"), lax.axis_size("grp")
    me_g = lax.axis_index("grp")
    width = tokens.shape[1]
    half = width // grp
    owner = width // (rep * grp)
    hid = weights.shape[2]
    peers = ep * grp
    rows = peers * CAP
    pad = 128
    f32, bf16 = jnp.float32, jnp.bfloat16
    match, combined, slot_map = route_slots(expert_ids, combine)
    slot_bf = slot_map.astype(bf16)
    xs = jnp.dot(slot_bf, tokens, preferred_element_type=f32).astype(bf16)
    ys = jnp.dot(slot_bf, grad_out, preferred_element_type=f32).astype(bf16)
    cs = jnp.sum(slot_map * combined[None, :], axis=1).astype(bf16)
    sent = jnp.concatenate([xs, ys, jnp.broadcast_to(cs[:, None], (CAP, pad))], axis=1)
    got = lax.all_gather(sent, ("grp", "ep"), axis=0, tiled=True)
    pair = got[:, : 2 * width].reshape(rows, 2, width)
    scale = got[:, 2 * width : 2 * width + 1].astype(f32)
    mine = lax.dynamic_slice_in_dim(pair, me_g * half, half, axis=2)
    blocks = pair.reshape(rows, 2, rep, grp, owner)
    blocks = lax.dynamic_index_in_dim(blocks, me_g, axis=3, keepdims=False)
    blocks = jnp.transpose(blocks, (2, 0, 1, 3)).reshape(rep, rows, 2 * owner)
    cols = lax.all_to_all(blocks, "rep", split_axis=0, concat_axis=0, tiled=True)
    cols = cols.reshape(rep * rows, 2, owner)
    w = jnp.transpose(weights, (1, 0, 2))
    pre = jnp.concatenate(
        [
            jnp.dot(mine[:, 0], w[0], preferred_element_type=f32),
            jnp.dot(mine[:, 0], w[1], preferred_element_type=f32),
            jnp.dot(mine[:, 1], w[2], preferred_element_type=f32),
        ],
        axis=1,
    )
    pre = lax.psum(pre, "grp")
    a, b, back = pre[:, :hid], pre[:, hid : 2 * hid], pre[:, 2 * hid :]
    sig = jax.nn.sigmoid(a)
    act = a * sig
    h = act * b
    dh = scale * back
    da = (dh * b * sig * (1.0 + a * (1.0 - sig))).astype(bf16)
    db = (dh * act).astype(bf16)
    hc = (scale * h).astype(bf16)
    pc = jnp.sum(h * back, axis=1, keepdims=True).astype(bf16)
    hidden = lax.all_gather(jnp.concatenate([da, db, hc], axis=1), "rep", axis=0, tiled=True)
    dn = (((1,), (1,)), ((), ()))
    px = lax.dot_general(da, w[0], dn, preferred_element_type=f32)
    px = (px + lax.dot_general(db, w[1], dn, preferred_element_type=f32)).astype(bf16)
    out = jnp.concatenate([px, jnp.broadcast_to(pc, (rows, pad))], axis=1)
    ret = lax.all_to_all(out, ("grp", "ep"), split_axis=0, concat_axis=0, tiled=True)
    ret = ret.reshape(grp, ep, CAP, half + pad).astype(f32)
    summed = jnp.sum(ret, axis=1)
    summed_x = jnp.transpose(summed[:, :, :half], (1, 0, 2)).reshape(CAP, width)
    summed_c = summed[0, :, half]
    highest = lax.Precision.HIGHEST
    tn = (((0,), (0,)), ((), ()))
    grad_tokens = lax.dot_general(slot_map, summed_x, tn, precision=highest).astype(bf16)
    per_token = jnp.sum(slot_map * summed_c[:, None], axis=0)
    grad_combine = match * per_token[:, None]
    gw = [
        lax.dot_general(cols[:, i], hidden[:, k * hid : (k + 1) * hid], tn, preferred_element_type=f32)
        for k, i in ((0, 0), (1, 0), (2, 1))
    ]
    return grad_tokens, grad_combine, jnp.stack(gw, axis=1)

CHUNK = 256
MESH = pl.DeviceIdType.MESH
F32, BF16 = jnp.float32, jnp.bfloat16


def pick(sources, piece, flip=False):
    shape = (sources * 16, sources * CAP) if flip else (sources * CAP, sources * 16)
    row = lax.broadcasted_iota(jnp.int32, shape, 1 if flip else 0)
    col = lax.broadcasted_iota(jnp.int32, shape, 0 if flip else 1)
    return (col == (row >> 2) * 16 + piece * CAP + (row & 3)).astype(F32).astype(BF16)


def mm(a, b):
    return jnp.dot(a, b, preferred_element_type=F32)


def mm_nt(a, b):
    return lax.dot_general(a, b, (((1,), (1,)), ((), ())), preferred_element_type=F32)


def exchange_kernel(
    dims, slots_ref, comb_ref, tok_ref, gout_ref, w_hbm, hid_ref, cols_ref, sum_ref,
    w_ref, sent, sent2, got, got2, part, psend, precv, back_s, back_r, acc,
    w_sem, g_sem, g2_sem, y_sem, x_sem, c_sem, f_sem, xc_sem, b_sem,
):
    rep, ep, grp, half, owner, hid = dims
    peers, rows, nch = ep * grp, ep * grp * CAP, hid // CHUNK
    hw, ow, qw = half // 2, owner // 2, half // 4
    r, j, g = lax.axis_index("rep"), lax.axis_index("ep"), lax.axis_index("grp")
    me = g * ep + j

    def peer(d):
        other = lax.rem(me + d, peers)
        return other, {"ep": lax.rem(other, ep), "grp": lax.div(other, ep)}

    def rep_peer(d):
        return lax.rem(r + d, rep)

    barrier = pltpu.get_barrier_semaphore()
    for d in range(1, peers):
        pl.semaphore_signal(barrier, inc=1, device_id=peer(d)[1], device_id_type=MESH)
    for d in range(1, rep):
        pl.semaphore_signal(barrier, inc=1, device_id={"rep": rep_peer(d)}, device_id_type=MESH)
    loads = [pltpu.make_async_copy(w_hbm.at[k], w_ref.at[k], w_sem.at[k]) for k in range(3)]
    for load in loads:
        load.start()

    srcs = (tok_ref, gout_ref)
    for gg in range(grp):
        total = jnp.zeros((16, hw), F32)
        for lohi in range(2):
            for xy in range(2):
                at = (gg * 2 + lohi) * hw
                total += mm(slots_ref[lohi * 2 + xy], srcs[xy][:, at : at + hw])
        sent[gg, :, 0:hw] = total.astype(BF16)
        sent[gg, :, hw : hw + 128] = mm(slots_ref[0], comb_ref[...]).astype(BF16)
    for gg in range(grp):
        for rr in range(rep):
            total = jnp.zeros((16, ow), F32)
            for lohi in range(2):
                for xy in range(2):
                    at = (rr * grp + gg) * owner + lohi * ow
                    total += mm(slots_ref[lohi * 2 + xy], srcs[xy][:, at : at + ow])
            sent2[gg, rr] = total.astype(BF16)
    pl.semaphore_wait(barrier, peers - 1 + rep - 1)

    gather, gather2 = [], []
    for out, src, dst, sem in ((gather, sent, got, g_sem), (gather2, sent2, got2, g2_sem)):
        for d in range(1, peers):
            other, where = peer(d)
            copy = pltpu.make_async_remote_copy(
                src_ref=src.at[lax.div(other, ep)], dst_ref=dst.at[me],
                send_sem=sem.at[0, d], recv_sem=sem.at[1, d],
                device_id=where, device_id_type=MESH,
            )
            copy.start()
            out.append(copy)
    got[me] = sent[g]
    got2[me] = sent2[g]
    for copy in gather:
        copy.wait_recv()
    flat = got[...].reshape(peers * 16, hw + 128)
    body = flat[:, :hw]
    x = jnp.concatenate([mm(pick(peers, 0), body), mm(pick(peers, 2), body)], axis=1).astype(BF16)
    y = jnp.concatenate([mm(pick(peers, 1), body), mm(pick(peers, 3), body)], axis=1).astype(BF16)
    scale = mm(pick(peers, 0), flat[:, hw:])[:, :1]
    for load in loads:
        load.wait()

    def across(c):
        return pltpu.make_async_remote_copy(
            src_ref=psend.at[c], dst_ref=precv.at[c],
            send_sem=y_sem.at[0, c], recv_sem=y_sem.at[1, c],
            device_id={"grp": 1 - g}, device_id_type=MESH,
        )

    def spread(c, who, sem, to):
        return pltpu.make_async_remote_copy(
            src_ref=hid_ref.at[who, c], dst_ref=hid_ref.at[who, c],
            send_sem=sem.at[0, c], recv_sem=sem.at[1, c],
            device_id={"rep": to}, device_id_type=MESH,
        )

    far, near = lax.rem(r + 2, rep), r + 1 - 2 * lax.rem(r, 2)

    @pl.loop(0, nch)
    def _(c):
        at = pl.ds(pl.multiple_of(c * CHUNK, CHUNK), CHUNK)
        for k in range(3):
            value = mm(y if k == 2 else x, w_ref[k, :, at])
            small = value.astype(BF16)
            part[c, k] = value
            psend[c, k] = small
        across(c).start()

    for copy in gather2:
        copy.wait_recv()
    moves = []
    for d in range(1, rep):
        to = rep_peer(d)
        copy = pltpu.make_async_remote_copy(
            src_ref=got2.at[:, to], dst_ref=cols_ref.at[r],
            send_sem=xc_sem.at[0, d], recv_sem=xc_sem.at[1, d],
            device_id={"rep": to}, device_id_type=MESH,
        )
        copy.start()
        moves.append(copy)
    for p in range(peers):
        cols_ref[r, p] = got2[p, r]
    acc[...] = jnp.zeros_like(acc)

    def step(c, sums):
        at = pl.ds(pl.multiple_of(c * CHUNK, CHUNK), CHUNK)
        across(c).wait_recv()
        own = [part[c, k] for k in range(3)]
        a, b, bk = [own[k] + precv[c, k].astype(F32) for k in range(3)]
        lost_a, lost_b, lost_bk = [own[k] - psend[c, k].astype(F32) for k in range(3)]
        sig = jax.nn.sigmoid(a)
        act = a * sig
        h = act * b
        slope_a = bk * b * sig * (1.0 + a * (1.0 - sig))
        slope_b = bk * act
        da = (scale * slope_a).astype(BF16)
        db = (scale * slope_b).astype(BF16)
        hid_ref[r, c, 0] = da
        hid_ref[r, c, 1] = db
        hid_ref[r, c, 2] = (scale * h).astype(BF16)
        spread(c, r, x_sem, far).start()
        spread(c, r, c_sem, near).start()
        acc[...] += mm_nt(da, w_ref[0, :, at]) + mm_nt(db, w_ref[1, :, at])

        @pl.when(c > 0)
        def _():
            spread(c - 1, far, x_sem, far).wait_recv()
            spread(c - 1, far, f_sem, near).start()

        fix = slope_a * lost_a + slope_b * lost_b + h * lost_bk
        return sums[0] + h * bk, sums[1] + fix

    wide = jnp.zeros((rows, CHUNK), F32)
    sums = lax.fori_loop(0, nch, step, (wide, wide))
    pc, fix = [jnp.sum(v, axis=1, keepdims=True) for v in sums]
    px = acc[...].astype(BF16)
    pcb = jnp.broadcast_to(pc, (rows, 128)).astype(BF16)
    fixb = jnp.broadcast_to(fix, (rows, 128)).astype(BF16)
    total = jnp.zeros((peers * 16, qw), F32)
    for q in range(4):
        total += mm(pick(peers, q, True), px[:, q * qw : (q + 1) * qw])
    back_s[:, :, 0:qw] = total.astype(BF16).reshape(peers, 16, qw)
    extra = mm(pick(peers, 0, True), pcb) + mm(pick(peers, 1, True), fixb)
    back_s[:, :, qw : qw + 128] = extra.astype(BF16).reshape(peers, 16, 128)
    returns = []
    for d in range(1, peers):
        other, where = peer(d)
        copy = pltpu.make_async_remote_copy(
            src_ref=back_s.at[other], dst_ref=back_r.at[me],
            send_sem=b_sem.at[0, d], recv_sem=b_sem.at[1, d],
            device_id=where, device_id_type=MESH,
        )
        copy.start()
        returns.append(copy)
    back_r[me] = back_s[me]
    spread(nch - 1, far, x_sem, far).wait_recv()
    spread(nch - 1, far, f_sem, near).start()
    for copy in returns:
        copy.wait_recv()
    for gg in range(grp):
        total = back_r[gg * ep].astype(F32)
        for jj in range(1, ep):
            total += back_r[gg * ep + jj].astype(F32)
        sum_ref[gg] = total

    for copy in gather + gather2 + returns:
        copy.wait_send()
    for copy in moves:
        copy.wait()

    @pl.loop(0, nch)
    def _(c):
        across(c).wait_send()
        spread(c, r, x_sem, far).wait_send()
        spread(c, r, c_sem, near).wait()
        spread(c, far, f_sem, near).wait()


def contract_kernel(cols_ref, hid_ref, sum_ref, slots_ref, gw_ref, gt_ref, xt):
    blocks, ow = cols_ref.shape[0] // 16, cols_ref.shape[1]

    @pl.when(pl.program_id(0) == 0)
    def _():
        for xy in range(2):
            both = [mm(pick(blocks, lohi * 2 + xy), cols_ref[...]) for lohi in range(2)]
            xt[xy] = jnp.concatenate(both, axis=1).T.astype(BF16)
        qw = sum_ref.shape[2] - 128
        for gg in range(sum_ref.shape[0]):
            rows = sum_ref[gg, :, 0:qw].astype(BF16)
            for q in range(4):
                at = (gg * 4 + q) * qw
                gt_ref[:, at : at + qw] = lax.dot_general(
                    slots_ref[q], rows, (((0,), (0,)), ((), ())), preferred_element_type=F32
                ).astype(BF16)

    for k in range(3):
        h = hid_ref[:, pl.program_id(0), k].reshape(-1, hid_ref.shape[4])
        gw_ref[k] = mm(xt[k // 2], h)


def direct(tokens, grad_out, expert_ids, combine, weights):
    ep, rep, grp = lax.axis_size("ep"), lax.axis_size("rep"), lax.axis_size("grp")
    count, width = tokens.shape
    half, owner, hid = width // grp, width // (rep * grp), weights.shape[2]
    peers, rows, nch = ep * grp, ep * grp * CAP, hid // CHUNK
    hw, ow, qw = half // 2, owner // 2, half // 4
    match, combined, slot_map = route_slots(expert_ids, combine)
    slots = jnp.stack([jnp.pad(slot_map, ((q * CAP, 12 - q * CAP), (0, 0))) for q in range(4)]).astype(BF16)
    comb = jnp.broadcast_to(combined[:, None], (count, 128)).astype(BF16)
    vmem = pl.BlockSpec(memory_space=pltpu.VMEM)
    dma = pltpu.SemaphoreType.DMA
    hidden, cols, sums = pl.pallas_call(
        functools.partial(exchange_kernel, (rep, ep, grp, half, owner, hid)),
        out_shape=(
            jax.ShapeDtypeStruct((rep, nch, 3, rows, CHUNK), BF16),
            jax.ShapeDtypeStruct((rep, peers, 16, ow), BF16),
            jax.ShapeDtypeStruct((grp, 16, qw + 128), F32),
        ),
        in_specs=[vmem] * 4 + [pl.BlockSpec(memory_space=pltpu.HBM)],
        out_specs=(vmem, vmem, vmem),
        scratch_shapes=[
            pltpu.VMEM((3, half, hid), BF16),
            pltpu.VMEM((grp, 16, hw + 128), BF16),
            pltpu.VMEM((grp, rep, 16, ow), BF16),
            pltpu.VMEM((peers, 16, hw + 128), BF16),
            pltpu.VMEM((peers, rep, 16, ow), BF16),
            pltpu.VMEM((nch, 3, rows, CHUNK), F32),
            pltpu.VMEM((nch, 3, rows, CHUNK), BF16),
            pltpu.VMEM((nch, 3, rows, CHUNK), BF16),
            pltpu.VMEM((peers, 16, qw + 128), BF16),
            pltpu.VMEM((peers, 16, qw + 128), BF16),
            pltpu.VMEM((rows, half), F32),
            dma((3,)),
            dma((2, peers)),
            dma((2, peers)),
            dma((2, nch)),
            dma((2, nch)),
            dma((2, nch)),
            dma((2, nch)),
            dma((2, rep)),
            dma((2, peers)),
        ],
        compiler_params=pltpu.CompilerParams(
            collective_id=0, has_side_effects=True, vmem_limit_bytes=40 << 20
        ),
    )(slots, comb, tokens, grad_out, jnp.transpose(weights, (1, 0, 2)))
    gw, grad_tokens = pl.pallas_call(
        contract_kernel,
        grid=(nch,),
        out_shape=(
            jax.ShapeDtypeStruct((3, owner, hid), F32),
            jax.ShapeDtypeStruct((count, width), BF16),
        ),
        in_specs=[vmem] * 4,
        out_specs=(
            pl.BlockSpec((3, owner, CHUNK), lambda c: (0, 0, c)),
            pl.BlockSpec((count, width), lambda c: (0, 0)),
        ),
        scratch_shapes=[pltpu.VMEM((2, owner, rep * rows), BF16)],
    )(cols.reshape(rep * peers * 16, ow), hidden, sums, slots)
    combine_sum = sums[0, :CAP, qw] + sums[1, CAP : 2 * CAP, qw]
    per_token = jnp.sum(slot_map * combine_sum[:, None], axis=0)
    return grad_tokens, match * per_token[:, None], jnp.transpose(gw, (1, 0, 2))


def solution(mesh):
    split = P(("rep", "ep", "grp"), None)
    in_specs = (split, split, split, split, P("grp", None, "ep"))
    out_specs = (split, split, P(("rep", "grp"), None, "ep"))
    sizes = dict(mesh.shape)

    def body(tokens, grad_out, expert_ids, combine, weights):
        owner = tokens.shape[1] // (sizes["rep"] * sizes["grp"])
        small = sizes["rep"] == 4 and sizes["grp"] == 2 and sizes["ep"] <= 8
        fits = owner % 256 == 0 and weights.shape[2] % CHUNK == 0
        run = direct if small and fits else local
        return run(tokens, grad_out, expert_ids, combine, weights)

    return jax.shard_map(body, mesh=mesh, in_specs=in_specs, out_specs=out_specs, check_vma=False)
```

```python
import functools

import jax
import jax.numpy as jnp
from jax import lax
from jax.experimental import pallas as pl
from jax.experimental.pallas import tpu as pltpu
from jax.sharding import PartitionSpec as P

FLIGHT = 1
CAP = 4


def route_slots(routing, gate_vals):
    match = (routing == 0).astype(jnp.float32)
    assigned = jnp.sum(match, axis=1)
    combined = jnp.sum(match * gate_vals.astype(jnp.float32), axis=1)
    before = jnp.cumsum(assigned) - assigned
    slot_index = jnp.arange(CAP, dtype=jnp.float32)
    slot_map = (before[None, :] == slot_index[:, None]).astype(jnp.float32) * assigned[None, :]
    return match, combined, slot_map


def local(tokens, grad_out, expert_ids, combine, weights):
    ep, rep, grp = lax.axis_size("ep"), lax.axis_size("rep"), lax.axis_size("grp")
    me_g = lax.axis_index("grp")
    width = tokens.shape[1]
    half = width // grp
    owner = width // (rep * grp)
    hid = weights.shape[2]
    peers = ep * grp
    rows = peers * CAP
    pad = 128
    f32, bf16 = jnp.float32, jnp.bfloat16
    match, combined, slot_map = route_slots(expert_ids, combine)
    slot_bf = slot_map.astype(bf16)
    xs = jnp.dot(slot_bf, tokens, preferred_element_type=f32).astype(bf16)
    ys = jnp.dot(slot_bf, grad_out, preferred_element_type=f32).astype(bf16)
    cs = jnp.sum(slot_map * combined[None, :], axis=1).astype(bf16)
    sent = jnp.concatenate([xs, ys, jnp.broadcast_to(cs[:, None], (CAP, pad))], axis=1)
    got = lax.all_gather(sent, ("grp", "ep"), axis=0, tiled=True)
    pair = got[:, : 2 * width].reshape(rows, 2, width)
    scale = got[:, 2 * width : 2 * width + 1].astype(f32)
    mine = lax.dynamic_slice_in_dim(pair, me_g * half, half, axis=2)
    blocks = pair.reshape(rows, 2, rep, grp, owner)
    blocks = lax.dynamic_index_in_dim(blocks, me_g, axis=3, keepdims=False)
    blocks = jnp.transpose(blocks, (2, 0, 1, 3)).reshape(rep, rows, 2 * owner)
    cols = lax.all_to_all(blocks, "rep", split_axis=0, concat_axis=0, tiled=True)
    cols = cols.reshape(rep * rows, 2, owner)
    w = jnp.transpose(weights, (1, 0, 2))
    pre = jnp.concatenate(
        [
            jnp.dot(mine[:, 0], w[0], preferred_element_type=f32),
            jnp.dot(mine[:, 0], w[1], preferred_element_type=f32),
            jnp.dot(mine[:, 1], w[2], preferred_element_type=f32),
        ],
        axis=1,
    )
    pre = lax.psum(pre, "grp")
    a, b, back = pre[:, :hid], pre[:, hid : 2 * hid], pre[:, 2 * hid :]
    sig = jax.nn.sigmoid(a)
    act = a * sig
    h = act * b
    dh = scale * back
    da = (dh * b * sig * (1.0 + a * (1.0 - sig))).astype(bf16)
    db = (dh * act).astype(bf16)
    hc = (scale * h).astype(bf16)
    pc = jnp.sum(h * back, axis=1, keepdims=True).astype(bf16)
    hidden = lax.all_gather(jnp.concatenate([da, db, hc], axis=1), "rep", axis=0, tiled=True)
    dn = (((1,), (1,)), ((), ()))
    px = lax.dot_general(da, w[0], dn, preferred_element_type=f32)
    px = (px + lax.dot_general(db, w[1], dn, preferred_element_type=f32)).astype(bf16)
    out = jnp.concatenate([px, jnp.broadcast_to(pc, (rows, pad))], axis=1)
    ret = lax.all_to_all(out, ("grp", "ep"), split_axis=0, concat_axis=0, tiled=True)
    ret = ret.reshape(grp, ep, CAP, half + pad).astype(f32)
    summed = jnp.sum(ret, axis=1)
    summed_x = jnp.transpose(summed[:, :, :half], (1, 0, 2)).reshape(CAP, width)
    summed_c = summed[0, :, half]
    highest = lax.Precision.HIGHEST
    tn = (((0,), (0,)), ((), ()))
    grad_tokens = lax.dot_general(slot_map, summed_x, tn, precision=highest).astype(bf16)
    per_token = jnp.sum(slot_map * summed_c[:, None], axis=0)
    grad_combine = match * per_token[:, None]
    gw = [
        lax.dot_general(cols[:, i], hidden[:, k * hid : (k + 1) * hid], tn, preferred_element_type=f32)
        for k, i in ((0, 0), (1, 0), (2, 1))
    ]
    return grad_tokens, grad_combine, jnp.stack(gw, axis=1)

CHUNK = 256
MESH = pl.DeviceIdType.MESH
F32, BF16 = jnp.float32, jnp.bfloat16


def pick(sources, piece, flip=False):
    shape = (sources * 16, sources * CAP) if flip else (sources * CAP, sources * 16)
    row = lax.broadcasted_iota(jnp.int32, shape, 1 if flip else 0)
    col = lax.broadcasted_iota(jnp.int32, shape, 0 if flip else 1)
    return (col == (row >> 2) * 16 + piece * CAP + (row & 3)).astype(F32).astype(BF16)


def mm(a, b):
    return jnp.dot(a, b, preferred_element_type=F32)


def mm_nt(a, b):
    return lax.dot_general(a, b, (((1,), (1,)), ((), ())), preferred_element_type=F32)


def exchange_kernel(
    dims, slots_ref, comb_ref, tok_ref, gout_ref, w_hbm, hid_ref, cols_ref, sum_ref,
    w_ref, sent, sent2, got, got2, part, psend, precv, back_s, back_r, acc,
    w_sem, g_sem, g2_sem, y_sem, x_sem, c_sem, f_sem, xc_sem, b_sem,
):
    rep, ep, grp, half, owner, hid = dims
    peers, rows, nch = ep * grp, ep * grp * CAP, hid // CHUNK
    hw, ow, qw = half // 2, owner // 2, half // 4
    r, j, g = lax.axis_index("rep"), lax.axis_index("ep"), lax.axis_index("grp")
    me = g * ep + j

    def peer(d):
        other = lax.rem(me + d, peers)
        return other, {"ep": lax.rem(other, ep), "grp": lax.div(other, ep)}

    def rep_peer(d):
        return lax.rem(r + d, rep)

    barrier = pltpu.get_barrier_semaphore()
    for d in range(1, peers):
        pl.semaphore_signal(barrier, inc=1, device_id=peer(d)[1], device_id_type=MESH)
    for d in range(1, rep):
        pl.semaphore_signal(barrier, inc=1, device_id={"rep": rep_peer(d)}, device_id_type=MESH)
    loads = [pltpu.make_async_copy(w_hbm.at[k], w_ref.at[k], w_sem.at[k]) for k in range(3)]
    for load in loads:
        load.start()

    srcs = (tok_ref, gout_ref)
    for gg in range(grp):
        total = jnp.zeros((16, hw), F32)
        for lohi in range(2):
            for xy in range(2):
                at = (gg * 2 + lohi) * hw
                total += mm(slots_ref[lohi * 2 + xy], srcs[xy][:, at : at + hw])
        sent[gg, :, 0:hw] = total.astype(BF16)
        sent[gg, :, hw : hw + 128] = mm(slots_ref[0], comb_ref[...]).astype(BF16)
    for gg in range(grp):
        for rr in range(rep):
            total = jnp.zeros((16, ow), F32)
            for lohi in range(2):
                for xy in range(2):
                    at = (rr * grp + gg) * owner + lohi * ow
                    total += mm(slots_ref[lohi * 2 + xy], srcs[xy][:, at : at + ow])
            sent2[gg, rr] = total.astype(BF16)
    pl.semaphore_wait(barrier, peers - 1 + rep - 1)

    gather, gather2 = [], []
    for out, src, dst, sem in ((gather, sent, got, g_sem), (gather2, sent2, got2, g2_sem)):
        for d in range(1, peers):
            other, where = peer(d)
            copy = pltpu.make_async_remote_copy(
                src_ref=src.at[lax.div(other, ep)], dst_ref=dst.at[me],
                send_sem=sem.at[0, d], recv_sem=sem.at[1, d],
                device_id=where, device_id_type=MESH,
            )
            copy.start()
            out.append(copy)
    got[me] = sent[g]
    got2[me] = sent2[g]
    for copy in gather:
        copy.wait_recv()
    flat = got[...].reshape(peers * 16, hw + 128)
    body = flat[:, :hw]
    x = jnp.concatenate([mm(pick(peers, 0), body), mm(pick(peers, 2), body)], axis=1).astype(BF16)
    y = jnp.concatenate([mm(pick(peers, 1), body), mm(pick(peers, 3), body)], axis=1).astype(BF16)
    scale = mm(pick(peers, 0), flat[:, hw:])[:, :1]
    for load in loads:
        load.wait()

    def across(c):
        return pltpu.make_async_remote_copy(
            src_ref=psend.at[c], dst_ref=precv.at[c],
            send_sem=y_sem.at[0, c], recv_sem=y_sem.at[1, c],
            device_id={"grp": 1 - g}, device_id_type=MESH,
        )

    def spread(c, who, sem, to):
        return pltpu.make_async_remote_copy(
            src_ref=hid_ref.at[who, c], dst_ref=hid_ref.at[who, c],
            send_sem=sem.at[0, c], recv_sem=sem.at[1, c],
            device_id={"rep": to}, device_id_type=MESH,
        )

    far, near = lax.rem(r + 2, rep), r + 1 - 2 * lax.rem(r, 2)

    @pl.loop(0, nch)
    def _(c):
        at = pl.ds(pl.multiple_of(c * CHUNK, CHUNK), CHUNK)
        for k in range(3):
            value = mm(y if k == 2 else x, w_ref[k, :, at])
            small = value.astype(BF16)
            part[c, k] = value
            psend[c, k] = small
        across(c).start()

    for copy in gather2:
        copy.wait_recv()
    moves = []
    for d in range(1, rep):
        to = rep_peer(d)
        copy = pltpu.make_async_remote_copy(
            src_ref=got2.at[:, to], dst_ref=cols_ref.at[r],
            send_sem=xc_sem.at[0, d], recv_sem=xc_sem.at[1, d],
            device_id={"rep": to}, device_id_type=MESH,
        )
        copy.start()
        moves.append(copy)
    for p in range(peers):
        cols_ref[r, p] = got2[p, r]
    acc[...] = jnp.zeros_like(acc)

    def step(c, sums):
        at = pl.ds(pl.multiple_of(c * CHUNK, CHUNK), CHUNK)
        across(c).wait_recv()
        own = [part[c, k] for k in range(3)]
        a, b, bk = [own[k] + precv[c, k].astype(F32) for k in range(3)]
        lost_a, lost_b, lost_bk = [own[k] - psend[c, k].astype(F32) for k in range(3)]
        sig = jax.nn.sigmoid(a)
        act = a * sig
        h = act * b
        slope_a = bk * b * sig * (1.0 + a * (1.0 - sig))
        slope_b = bk * act
        da = (scale * slope_a).astype(BF16)
        db = (scale * slope_b).astype(BF16)
        hid_ref[r, c, 0] = da
        hid_ref[r, c, 1] = db
        hid_ref[r, c, 2] = (scale * h).astype(BF16)
        spread(c, r, x_sem, far).start()
        spread(c, r, c_sem, near).start()
        acc[...] += mm_nt(da, w_ref[0, :, at]) + mm_nt(db, w_ref[1, :, at])

        @pl.when(c > 0)
        def _():
            spread(c - 1, far, x_sem, far).wait_recv()
            spread(c - 1, far, f_sem, near).start()

        fix = slope_a * lost_a + slope_b * lost_b + h * lost_bk
        return sums[0] + h * bk, sums[1] + fix

    wide = jnp.zeros((rows, CHUNK), F32)
    sums = lax.fori_loop(0, nch, step, (wide, wide))
    pc, fix = [jnp.sum(v, axis=1, keepdims=True) for v in sums]
    px = acc[...].astype(BF16)
    pcb = jnp.broadcast_to(pc, (rows, 128)).astype(BF16)
    fixb = jnp.broadcast_to(fix, (rows, 128)).astype(BF16)
    total = jnp.zeros((peers * 16, qw), F32)
    for q in range(4):
        total += mm(pick(peers, q, True), px[:, q * qw : (q + 1) * qw])
    back_s[:, :, 0:qw] = total.astype(BF16).reshape(peers, 16, qw)
    extra = mm(pick(peers, 0, True), pcb) + mm(pick(peers, 1, True), fixb)
    back_s[:, :, qw : qw + 128] = extra.astype(BF16).reshape(peers, 16, 128)
    returns = []
    for d in range(1, peers):
        other, where = peer(d)
        copy = pltpu.make_async_remote_copy(
            src_ref=back_s.at[other], dst_ref=back_r.at[me],
            send_sem=b_sem.at[0, d], recv_sem=b_sem.at[1, d],
            device_id=where, device_id_type=MESH,
        )
        copy.start()
        returns.append(copy)
    back_r[me] = back_s[me]
    spread(nch - 1, far, x_sem, far).wait_recv()
    spread(nch - 1, far, f_sem, near).start()
    for copy in returns:
        copy.wait_recv()
    for gg in range(grp):
        total = back_r[gg * ep].astype(F32)
        for jj in range(1, ep):
            total += back_r[gg * ep + jj].astype(F32)
        sum_ref[gg] = total

    for copy in gather + gather2 + returns:
        copy.wait_send()
    for copy in moves:
        copy.wait()

    @pl.loop(0, nch)
    def _(c):
        across(c).wait_send()
        spread(c, r, x_sem, far).wait_send()
        spread(c, r, c_sem, near).wait()
        spread(c, far, f_sem, near).wait()


def contract_kernel(cols_ref, hid_ref, sum_ref, slots_ref, gw_ref, gt_ref, xt):
    blocks, ow = cols_ref.shape[0] // 16, cols_ref.shape[1]

    @pl.when(pl.program_id(0) == 0)
    def _():
        for xy in range(2):
            both = [mm(pick(blocks, lohi * 2 + xy), cols_ref[...]) for lohi in range(2)]
            xt[xy] = jnp.concatenate(both, axis=1).T.astype(BF16)
        qw = sum_ref.shape[2] - 128
        for gg in range(sum_ref.shape[0]):
            rows = sum_ref[gg, :, 0:qw].astype(BF16)
            for q in range(4):
                at = (gg * 4 + q) * qw
                gt_ref[:, at : at + qw] = lax.dot_general(
                    slots_ref[q], rows, (((0,), (0,)), ((), ())), preferred_element_type=F32
                ).astype(BF16)

    for k in range(3):
        h = hid_ref[:, pl.program_id(0), k].reshape(-1, hid_ref.shape[4])
        gw_ref[k] = mm(xt[k // 2], h)


def direct(tokens, grad_out, expert_ids, combine, weights):
    ep, rep, grp = lax.axis_size("ep"), lax.axis_size("rep"), lax.axis_size("grp")
    count, width = tokens.shape
    half, owner, hid = width // grp, width // (rep * grp), weights.shape[2]
    peers, rows, nch = ep * grp, ep * grp * CAP, hid // CHUNK
    hw, ow, qw = half // 2, owner // 2, half // 4
    match, combined, slot_map = route_slots(expert_ids, combine)
    slots = jnp.stack([jnp.pad(slot_map, ((q * CAP, 12 - q * CAP), (0, 0))) for q in range(4)]).astype(BF16)
    comb = jnp.broadcast_to(combined[:, None], (count, 128)).astype(BF16)
    vmem = pl.BlockSpec(memory_space=pltpu.VMEM)
    dma = pltpu.SemaphoreType.DMA
    hidden, cols, sums = pl.pallas_call(
        functools.partial(exchange_kernel, (rep, ep, grp, half, owner, hid)),
        out_shape=(
            jax.ShapeDtypeStruct((rep, nch, 3, rows, CHUNK), BF16),
            jax.ShapeDtypeStruct((rep, peers, 16, ow), BF16),
            jax.ShapeDtypeStruct((grp, 16, qw + 128), F32),
        ),
        in_specs=[vmem] * 4 + [pl.BlockSpec(memory_space=pltpu.HBM)],
        out_specs=(vmem, vmem, vmem),
        scratch_shapes=[
            pltpu.VMEM((3, half, hid), BF16),
            pltpu.VMEM((grp, 16, hw + 128), BF16),
            pltpu.VMEM((grp, rep, 16, ow), BF16),
            pltpu.VMEM((peers, 16, hw + 128), BF16),
            pltpu.VMEM((peers, rep, 16, ow), BF16),
            pltpu.VMEM((nch, 3, rows, CHUNK), F32),
            pltpu.VMEM((nch, 3, rows, CHUNK), BF16),
            pltpu.VMEM((nch, 3, rows, CHUNK), BF16),
            pltpu.VMEM((peers, 16, qw + 128), BF16),
            pltpu.VMEM((peers, 16, qw + 128), BF16),
            pltpu.VMEM((rows, half), F32),
            dma((3,)),
            dma((2, peers)),
            dma((2, peers)),
            dma((2, nch)),
            dma((2, nch)),
            dma((2, nch)),
            dma((2, nch)),
            dma((2, rep)),
            dma((2, peers)),
        ],
        compiler_params=pltpu.CompilerParams(
            collective_id=0, has_side_effects=True, vmem_limit_bytes=60 << 20
        ),
    )(slots, comb, tokens, grad_out, jnp.transpose(weights, (1, 0, 2)))
    gw, grad_tokens = pl.pallas_call(
        contract_kernel,
        grid=(nch,),
        out_shape=(
            jax.ShapeDtypeStruct((3, owner, hid), F32),
            jax.ShapeDtypeStruct((count, width), BF16),
        ),
        in_specs=[vmem] * 4,
        out_specs=(
            pl.BlockSpec((3, owner, CHUNK), lambda c: (0, 0, c)),
            pl.BlockSpec((count, width), lambda c: (0, 0)),
        ),
        scratch_shapes=[pltpu.VMEM((2, owner, rep * rows), BF16)],
    )(cols.reshape(rep * peers * 16, ow), hidden, sums, slots)
    combine_sum = sums[0, :CAP, qw] + sums[1, CAP : 2 * CAP, qw]
    per_token = jnp.sum(slot_map * combine_sum[:, None], axis=0)
    return grad_tokens, match * per_token[:, None], jnp.transpose(gw, (1, 0, 2))


def solution(mesh):
    split = P(("rep", "ep", "grp"), None)
    in_specs = (split, split, split, split, P("grp", None, "ep"))
    out_specs = (split, split, P(("rep", "grp"), None, "ep"))
    sizes = dict(mesh.shape)

    def body(tokens, grad_out, expert_ids, combine, weights):
        owner = tokens.shape[1] // (sizes["rep"] * sizes["grp"])
        small = sizes["rep"] == 4 and sizes["grp"] == 2 and sizes["ep"] <= 8
        fits = owner % 256 == 0 and weights.shape[2] % CHUNK == 0
        run = direct if small and fits else local
        return run(tokens, grad_out, expert_ids, combine, weights)

    return jax.shard_map(body, mesh=mesh, in_specs=in_specs, out_specs=out_specs, check_vma=False)
```
